1024 devices in a mesh: grp: 16 (over z, core), dev: 64 (over x, y).
Axes of the slice: x: 8, y: 8, z: 8, core: 2. Of those that a mesh axis runs over, the one named last changes fastest.
Arguments:
- orbitals: bfloat16 [16, 64, 64, 2, 2304], P('grp', 'dev'), may hold values from -6 to 6
- potential: bfloat16 [64, 2304], P('dev'), may hold values from -4 to 4
- counts: int32 [16, 64], P('grp'), may hold values from 16 to 64, as said below
- parity: int32 [16, 64], P('grp', 'dev'), may hold values 0 or 1
Outputs:
- density: float32 [64, 1, 2304], P('dev', None, 'grp')
- filtered: bfloat16 [16, 64, 64, 2, 2304], P('grp', 'dev')
The draws below stay inside these ranges and needn't reach their ends.
Inputs may be any that keep to these rules, and one draw needn't show every extreme that they name: In each row of 64 fragments the counts sum to 1792, and some fragment of every row holds 64 orbitals and some holds 16.
All inputs are finite; a program needn't handle non-finite values. No bound on the sum of `parity` on one device may be relied on, other than what follows from the above.
Results may differ from the reference program's by a relative error of at most 0.0026.
Values may be sent and summed in bfloat16 or wider, within the bound.
A program may use at most 32 MiB of HBM per device.

```python
import jax
import jax.numpy as jnp
from jax import lax

MAXORB = 64
MINORB = 16
DEGREE = 8
BX = 1
BY = 48
BZ = 48
N_GRP = 16
N_DEV = 64


def draw_counts(key, part):
    spread = MAXORB - MINORB
    quads = N_DEV // 4

    def one_group(group_key):
        key_order, key_cuts = jax.random.split(group_key)
        order = jax.random.permutation(key_order, N_DEV)
        cuts = jnp.sort(jax.random.randint(key_cuts, (quads, 3), 0, spread + 1), axis=1)
        cuts = jnp.where(jnp.arange(quads)[:, None] == 0, 0, cuts)
        edges = jnp.concatenate([jnp.zeros((quads, 1), jnp.int32), cuts.astype(jnp.int32), jnp.full((quads, 1), spread, jnp.int32)], 1)
        pieces = (edges[:, 1:] - edges[:, :-1]).reshape(-1)
        values = MINORB + pieces
        return values[jnp.argsort(order)].astype(jnp.int32)
    group_keys = jax.random.split(jax.random.fold_in(key, 17), N_GRP)
    return jax.vmap(one_group)(group_keys)


def place_ends(array, stream_key, smallest, top_value):
    longest = array.shape.index(max(array.shape))
    spots = []
    for shift in (0, 1):
        where = [jax.random.randint(jax.random.fold_in(stream_key, axis), (), 0, length) for axis, length in enumerate(array.shape)]
        where[longest] = (where[longest] + shift) % array.shape[longest]
        spots.append(tuple(where))
    return array.at[spots[0]].set(smallest).at[spots[1]].set(top_value)


def steps_of(rng, shape, shards, low, top_value):
    def one(position, shards_of):
        heights = jax.random.uniform(jax.random.fold_in(jax.random.fold_in(rng, 6), position), (shards_of,), jnp.float32, low / len(shards), top_value / len(shards))
        return jnp.repeat(jnp.exp(heights), shape[position] // shards_of).reshape((-1,) + (1,) * (len(shape) - position - 1))

    factor_of = one(*shards[0])
    for cut in shards[1:]:
        factor_of = factor_of * one(*cut)
    return factor_of


def bell_draw(key, shape, scale, bound, cuts=(), kind=jnp.bfloat16):
    factor_of = steps_of(key, shape, cuts, -0.22, 0.18) if cuts else 1.0
    values = jax.random.normal(key, shape, jnp.float32) * scale * factor_of
    return jnp.minimum(jnp.maximum(values, -bound), bound).astype(kind)


def setup_inputs(seed: int = 0) -> dict:
    keys = jax.random.split(jax.random.key(seed), 5)
    orbitals = bell_draw(keys[0], (N_GRP, N_DEV, MAXORB, 2 * BX, BY * BZ), 1.0, 6.0, ((0, 16), (1, 64)))
    potential = bell_draw(keys[1], (N_DEV * BX, BY * BZ), 1.0, 4.0, ((0, 64),))
    counts = draw_counts(jax.random.fold_in(keys[4], 71), 0)
    parity = place_ends((jax.random.randint(keys[3], (N_GRP, N_DEV), 0, 2) < 1).astype(jnp.int32), jax.random.fold_in(keys[3], 1), 0, 1)
    return {"orbitals": orbitals, "potential": potential, "counts": counts, "parity": parity}


filter_centre = 9.0
filter_half = 7.0

def beside_sum(field):
    edge_x = jnp.zeros_like(field[:, :1])
    along_x = jnp.concatenate([field[:, 1:], edge_x], 1) + jnp.concatenate([edge_x, field[:, :-1]], 1)
    edge_y = jnp.zeros_like(field[:, :, :BZ])
    along_y = jnp.concatenate([field[:, :, BZ:], edge_y], 2) + jnp.concatenate([edge_y, field[:, :, :-BZ]], 2)
    edge_z = jnp.zeros_like(field[:, :, :1])
    upper = jnp.concatenate([field[:, :, 1:], edge_z], 2)
    lower = jnp.concatenate([edge_z, field[:, :, :-1]], 2)
    z_index = jnp.arange(field.shape[2]) % BZ
    along_z = jnp.where(z_index == BZ - 1, 0.0, upper) + jnp.where(z_index == 0, 0.0, lower)
    return along_x + along_y + along_z

def step_map(field, patches):
    return (6.0 * field - beside_sum(field) + patches * field - filter_centre * field) / filter_half

def chebyshev_rows(orbital_rows, patches):
    previous = orbital_rows.astype(jnp.float32)
    current = step_map(previous, patches)
    for degree_step in range(DEGREE - 1):
        previous, current = (current, 2.0 * step_map(current, patches) - previous)
    mean_square = lax.optimization_barrier(jnp.mean(current * current, axis=(1, 2), keepdims=True))
    return (current * lax.rsqrt(mean_square + 1e-06)).astype(jnp.bfloat16)

def reference(orbitals, potential, counts, parity):
    blocks = potential.astype(jnp.float32).reshape(N_DEV, BX, BY * BZ)
    patches = jnp.concatenate([blocks, jnp.roll(blocks, -1, axis=0)], axis=1)
    patches = jnp.tile(patches, (N_GRP, 1, 1))
    slot_ids = jnp.arange(MAXORB, dtype=jnp.int32)

    def fragment(inputs):
        orbital_rows, own_patch, my_count, parity_bit = inputs
        result = chebyshev_rows(orbital_rows, own_patch[None])
        result = jnp.where((slot_ids < my_count)[:, None, None], result, jnp.zeros((), jnp.bfloat16))
        squares = result.astype(jnp.float32)
        density_part = lax.optimization_barrier(jnp.sum(squares * squares, axis=0)) * ((1.0 - 2.0 * parity_bit.astype(jnp.float32)) / MAXORB)
        return (result, density_part)
    stacked = orbitals.reshape(N_GRP * N_DEV, MAXORB, 2 * BX, BY * BZ)
    results, parts = lax.map(fragment, (stacked, patches, counts.reshape(-1), parity.reshape(-1)))
    totals = lax.optimization_barrier(jnp.sum(parts.reshape(N_GRP, N_DEV, 2, BX, BY * BZ), axis=0))
    density = totals[:, 0] + jnp.roll(totals[:, 1], 1, axis=0)
    return (density, results.reshape(orbitals.shape))
```

```python
import functools
import math

import jax
import jax.numpy as jnp
from jax import lax
from jax.experimental import pallas as pl
from jax.experimental.pallas import tpu as pltpu
from jax.sharding import PartitionSpec as P

MAXORB = 64
CELLS = 2304
BZ = 48
ROWS = 48
BANDS = 6
TILES = 18
LANES = 128
SHARE = 144
GRP = 16
DEV = 64
ROOTS = [math.cos((2 * i - 1) * math.pi / 16) for i in (1, 8, 4, 5, 2, 7, 3, 6)]
LEAD = 2.0**7 / 7.0**8
MESH = pl.DeviceIdType.MESH
F32 = jnp.float32
BF16 = jnp.bfloat16


def iota(shape, dim):
    return lax.broadcasted_iota(jnp.int32, shape, dim)


def slot_matrix():
    row, lane = iota((LANES, LANES), 0), iota((LANES, LANES), 1)
    return jnp.where((row >> 1) + (row & 1) * MAXORB == lane, 1.0, 0.0).astype(BF16)


def band(ref, y, zi):
    return ref[pl.ds(y * BZ + zi, 8, stride=BANDS), :]


def factor(field, weight, root, with_sum):
    sub = iota((8, LANES), 0)
    first, last = sub == 0, sub == 7
    shift = 7.0 * root
    zero = jnp.zeros((8, LANES), F32)
    before, here = [zero] * BANDS, [band(field, 0, z) for z in range(BANDS)]
    total = zero
    for y in range(ROWS):
        after = [band(field, y + 1, z) for z in range(BANDS)] if y + 1 < ROWS else [zero] * BANDS
        low = jnp.where(first, 0.0, pltpu.roll(here[-1], 1, 0))
        high = jnp.where(last, 0.0, pltpu.roll(here[0], 7, 0))
        wide = [low] + here + [high]
        for z in range(BANDS):
            beside = (wide[z] + wide[z + 2]) + (before[z] + after[z]) + pltpu.roll(here[z], MAXORB, 1)
            out = (band(weight, y, z) - shift) * here[z] - beside
            field[pl.ds(y * BZ + z, 8, stride=BANDS), :] = out
            if with_sum:
                total = total + out * out
        before, here = here, after
    return total


def root_at(k):
    value = jnp.float32(ROOTS[0])
    for i in range(1, len(ROOTS) - 1):
        value = jnp.where(k == i, jnp.float32(ROOTS[i]), value)
    return value


def local_weights(first, second, weight):
    row = iota((16, CELLS), 0)
    stacked = jnp.where(row == 0, first.astype(F32), jnp.where(row == 1, second.astype(F32), jnp.where(row == 2, 1.0, 0.0)))
    stacked = stacked.astype(BF16)
    row, lane = iota((16, LANES), 0), iota((16, LANES), 1)
    spread = jnp.where(row == 2, -3.0, jnp.where((row < 2) & (row == (lane >> 6)), 1.0, 0.0)).astype(BF16)
    for j in range(TILES):
        at = slice(j * LANES, (j + 1) * LANES)
        weight[at, :] = lax.dot_general(
            stacked[:, at], spread, (((0,), (0,)), ((), ())), preferred_element_type=F32
        )


def kernel(
    counts, parity, potential, orbitals, density, filtered,
    loaded, stored, field, weight, next_block, patch, outgoing, incoming,
    load_sem, store_sem, block_sem, send_sem, recv_sem,
):
    g, d = lax.axis_index("grp"), lax.axis_index("dev")
    ahead, behind = lax.rem(d + 1, DEV), lax.rem(d + DEV - 1, DEV)

    def other(k):
        return lax.rem(g + k, GRP)

    loads = [
        pltpu.make_async_copy(orbitals.at[:, :, pl.ds(j * LANES, LANES)], loaded.at[j], load_sem.at[j])
        for j in range(TILES)
    ]
    for copy in loads:
        copy.start()

    barrier = pltpu.get_barrier_semaphore()
    pl.semaphore_signal(barrier, inc=1, device_id=(g, ahead), device_id_type=MESH)

    def greet(k, carry):
        pl.semaphore_signal(barrier, inc=1, device_id=(other(k), behind), device_id_type=MESH)

        @pl.when(k > 0)
        def _():
            pl.semaphore_signal(barrier, inc=1, device_id=(other(k), d), device_id_type=MESH)

        return carry

    lax.fori_loop(0, GRP, greet, 0)

    slots = slot_matrix()
    for copy in loads:
        copy.wait()
    for j in range(TILES):
        tile = loaded[j].reshape(LANES, LANES)
        field[j * LANES : (j + 1) * LANES, :] = lax.dot_general(
            tile, slots, (((0,), (0,)), ((), ())), preferred_element_type=F32
        )

    pl.semaphore_wait(barrier, 2 * GRP)
    block = pltpu.make_async_remote_copy(
        src_ref=potential, dst_ref=next_block, send_sem=block_sem.at[0], recv_sem=block_sem.at[1],
        device_id=(g, behind), device_id_type=MESH,
    )
    block.start()
    block.wait()
    local_weights(potential[...], next_block[...], weight)

    def one(k, carry):
        factor(field, weight, root_at(k), False)
        return carry

    lax.fori_loop(0, len(ROOTS) - 1, one, 0)
    total = factor(field, weight, ROOTS[-1], True)
    total = jnp.sum(total, axis=0, keepdims=True)
    total = total + pltpu.roll(total, MAXORB, 1)
    scale = LEAD * lax.rsqrt(total * (LEAD * LEAD / (2 * CELLS)) + 1e-6)
    live = (iota((1, LANES), 1) & (MAXORB - 1)) < counts[0, d]
    sign = (1 - 2 * parity[0, 0]).astype(F32) / MAXORB

    stores = []
    for j in range(TILES):
        at = slice(j * LANES, (j + 1) * LANES)
        scaled = jnp.where(live, field[at, :] * scale, 0.0).astype(BF16)
        rows = lax.dot_general(slots, scaled, (((1,), (1,)), ((), ())), preferred_element_type=F32)
        stored[j] = rows.astype(BF16).reshape(MAXORB, 2, LANES)
        parts = [rows[8 * i : 8 * i + 8] for i in range(16)]
        parts = [p * p for p in parts]
        while len(parts) > 1:
            parts = [parts[i] + parts[i + 1] for i in range(0, len(parts), 2)]
        dens = parts[0]
        dens = dens + pltpu.roll(dens, 4, 0)
        dens = dens + pltpu.roll(dens, 2, 0)
        patch[:, at] = dens[0:2] * sign
    for j in range(TILES):
        copy = pltpu.make_async_copy(stored.at[j], filtered.at[:, :, pl.ds(j * LANES, LANES)], store_sem.at[j])
        copy.start()
        stores.append(copy)
    for k in range(GRP):
        piece = patch[:, k * SHARE : (k + 1) * SHARE]
        outgoing[0, k] = piece[0:1]
        outgoing[1, k] = piece[1:2]

    def send(kind, k):
        to, there = other(k), (d if kind == 0 else ahead)
        return pltpu.make_async_remote_copy(
            src_ref=outgoing.at[kind, to], dst_ref=incoming.at[kind, g],
            send_sem=send_sem.at[kind, to], recv_sem=recv_sem.at[kind, g],
            device_id=(to, there), device_id_type=MESH,
        )

    def arrival(kind, k):
        source = other(k)
        return pltpu.make_async_remote_copy(
            src_ref=outgoing.at[kind, source], dst_ref=incoming.at[kind, source],
            send_sem=send_sem.at[kind, source], recv_sem=recv_sem.at[kind, source],
            device_id=(source, d), device_id_type=MESH,
        )

    def start(k, carry):
        send(1, k).start()

        @pl.when(k > 0)
        def _():
            send(0, k).start()

        return carry

    lax.fori_loop(0, GRP, start, 0)

    def land(k, carry):
        arrival(1, k).wait_recv()

        @pl.when(k > 0)
        def _():
            arrival(0, k).wait_recv()

        return carry

    lax.fori_loop(0, GRP, land, 0)
    incoming[0, g] = outgoing[0, g]
    density[...] = jnp.sum(incoming[0], axis=0) + jnp.sum(incoming[1], axis=0)

    def leave(k, carry):
        send(1, k).wait_send()

        @pl.when(k > 0)
        def _():
            send(0, k).wait_send()

        return carry

    lax.fori_loop(0, GRP, leave, 0)
    for copy in stores:
        copy.wait()


def on_device(orbitals, potential, counts, parity):
    vmem = pl.BlockSpec(memory_space=pltpu.VMEM)
    smem = pl.BlockSpec(memory_space=pltpu.SMEM)
    hbm = pl.BlockSpec(memory_space=pl.ANY)
    density, filtered = pl.pallas_call(
        kernel,
        in_specs=[smem, smem, vmem, hbm],
        out_specs=[vmem, hbm],
        out_shape=[
            jax.ShapeDtypeStruct((1, SHARE), F32),
            jax.ShapeDtypeStruct((MAXORB, 2, CELLS), BF16),
        ],
        scratch_shapes=[
            pltpu.VMEM((TILES, MAXORB, 2, LANES), BF16),
            pltpu.VMEM((TILES, MAXORB, 2, LANES), BF16),
            pltpu.VMEM((CELLS, LANES), F32),
            pltpu.VMEM((CELLS, LANES), F32),
            pltpu.VMEM((1, CELLS), BF16),
            pltpu.VMEM((2, CELLS), F32),
            pltpu.VMEM((2, GRP, 1, SHARE), F32),
            pltpu.VMEM((2, GRP, 1, SHARE), F32),
            pltpu.SemaphoreType.DMA((TILES,)),
            pltpu.SemaphoreType.DMA((TILES,)),
            pltpu.SemaphoreType.DMA((2,)),
            pltpu.SemaphoreType.DMA((2, GRP)),
            pltpu.SemaphoreType.DMA((2, GRP)),
        ],
        compiler_params=pltpu.CompilerParams(collective_id=0, has_side_effects=True),
        name="filter_and_assemble",
    )(counts, parity, potential, orbitals[0, 0])
    return density[None], filtered[None, None]


def solution(mesh):
    placed = (P("grp", "dev", None, None, None), P("dev", None), P("grp", None), P("grp", "dev"))
    return jax.shard_map(
        on_device,
        mesh=mesh,
        in_specs=placed,
        out_specs=(P("dev", None, "grp"), P("grp", "dev", None, None, None)),
        check_vma=False,
    )
```

```python
import functools
import math

import jax
import jax.numpy as jnp
from jax import lax
from jax.experimental import pallas as pl
from jax.experimental.pallas import tpu as pltpu
from jax.sharding import PartitionSpec as P

MAXORB = 64
CELLS = 2304
BZ = 48
ROWS = 48
BANDS = 6
TILES = 18
LANES = 128
SHARE = 144
GRP = 16
DEV = 64
ROOTS = [math.cos((2 * i - 1) * math.pi / 16) for i in (1, 8, 4, 5, 2, 7, 3, 6)]
LEAD = 2.0**7 / 7.0**8
MESH = pl.DeviceIdType.MESH
F32 = jnp.float32
BF16 = jnp.bfloat16


def iota(shape, dim):
    return lax.broadcasted_iota(jnp.int32, shape, dim)


def slot_matrix():
    row, lane = iota((LANES, LANES), 0), iota((LANES, LANES), 1)
    return jnp.where((row >> 1) + (row & 1) * MAXORB == lane, 1.0, 0.0).astype(BF16)


def band(ref, y, zi):
    return ref[pl.ds(y * BZ + zi, 8, stride=BANDS), :]


def factor(field, weight, root, with_sum):
    sub = iota((8, LANES), 0)
    first, last = sub == 0, sub == 7
    shift = 7.0 * root
    zero = jnp.zeros((8, LANES), F32)
    before, here = [zero] * BANDS, [band(field, 0, z) for z in range(BANDS)]
    total = zero
    for y in range(ROWS):
        after = [band(field, y + 1, z) for z in range(BANDS)] if y + 1 < ROWS else [zero] * BANDS
        low = jnp.where(first, 0.0, pltpu.roll(here[-1], 1, 0))
        high = jnp.where(last, 0.0, pltpu.roll(here[0], 7, 0))
        wide = [low] + here + [high]
        for z in range(BANDS):
            beside = (wide[z] + wide[z + 2]) + (before[z] + after[z]) + pltpu.roll(here[z], MAXORB, 1)
            out = (band(weight, y, z) - shift) * here[z] - beside
            field[pl.ds(y * BZ + z, 8, stride=BANDS), :] = out
            if with_sum:
                total = total + out * out
        before, here = here, after
    return total


def local_weights(first, second, weight):
    row = iota((16, CELLS), 0)
    stacked = jnp.where(row == 0, first.astype(F32), jnp.where(row == 1, second.astype(F32), jnp.where(row == 2, 1.0, 0.0)))
    stacked = stacked.astype(BF16)
    row, lane = iota((16, LANES), 0), iota((16, LANES), 1)
    spread = jnp.where(row == 2, -3.0, jnp.where((row < 2) & (row == (lane >> 6)), 1.0, 0.0)).astype(BF16)
    for j in range(TILES):
        at = slice(j * LANES, (j + 1) * LANES)
        weight[at, :] = lax.dot_general(
            stacked[:, at], spread, (((0,), (0,)), ((), ())), preferred_element_type=F32
        )


def kernel(
    counts, parity, potential, orbitals, density, stored,
    loaded, field, weight, own, next_block, patch, outgoing, incoming, count_row, parity_bit,
    load_sem, small_sem, block_sem, send_sem, recv_sem,
):
    g, d = lax.axis_index("grp"), lax.axis_index("dev")
    ahead, behind = lax.rem(d + 1, DEV), lax.rem(d + DEV - 1, DEV)

    def other(k):
        return lax.rem(g + k, GRP)

    barrier = pltpu.get_barrier_semaphore()
    pl.semaphore_signal(barrier, inc=1, device_id=(g, ahead), device_id_type=MESH)

    def greet(k, carry):
        pl.semaphore_signal(barrier, inc=1, device_id=(other(k), behind), device_id_type=MESH)

        @pl.when(k > 0)
        def _():
            pl.semaphore_signal(barrier, inc=1, device_id=(other(k), d), device_id_type=MESH)

        return carry

    lax.fori_loop(0, GRP, greet, 0)

    small = [
        pltpu.make_async_copy(potential, own, small_sem.at[0]),
        pltpu.make_async_copy(counts, count_row, small_sem.at[1]),
        pltpu.make_async_copy(parity, parity_bit, small_sem.at[2]),
    ]
    for copy in small:
        copy.start()
    loads = [
        pltpu.make_async_copy(orbitals.at[:, :, pl.ds(j * LANES, LANES)], loaded.at[j], load_sem.at[j])
        for j in range(TILES)
    ]
    for copy in loads:
        copy.start()

    small[0].wait()
    pl.semaphore_wait(barrier, 2 * GRP)
    block = pltpu.make_async_remote_copy(
        src_ref=own, dst_ref=next_block, send_sem=block_sem.at[0], recv_sem=block_sem.at[1],
        device_id=(g, behind), device_id_type=MESH,
    )
    block.start()

    slots = slot_matrix()
    for copy in loads:
        copy.wait()
    for j in range(TILES):
        tile = loaded[j].reshape(LANES, LANES)
        field[j * LANES : (j + 1) * LANES, :] = lax.dot_general(
            tile, slots, (((0,), (0,)), ((), ())), preferred_element_type=F32
        )

    block.wait_recv()
    local_weights(own[...], next_block[...], weight)

    for root in ROOTS[:-1]:
        factor(field, weight, root, False)
    total = factor(field, weight, ROOTS[-1], True)
    total = jnp.sum(total, axis=0, keepdims=True)
    total = total + pltpu.roll(total, MAXORB, 1)
    scale = LEAD * lax.rsqrt(total * (LEAD * LEAD / (2 * CELLS)) + 1e-6)
    small[1].wait()
    small[2].wait()
    live = (iota((1, LANES), 1) & (MAXORB - 1)) < count_row[0, d]
    sign = (1 - 2 * parity_bit[0, 0]).astype(F32) / MAXORB

    def send(kind, k):
        there = d if kind == 0 else ahead
        return pltpu.make_async_remote_copy(
            src_ref=outgoing.at[kind, k], dst_ref=incoming.at[kind, g],
            send_sem=send_sem.at[kind, k], recv_sem=recv_sem.at[kind, g],
            device_id=(k, there), device_id_type=MESH,
        )

    def arrival(kind, source):
        return pltpu.make_async_remote_copy(
            src_ref=outgoing.at[kind, source], dst_ref=incoming.at[kind, source],
            send_sem=send_sem.at[kind, source], recv_sem=recv_sem.at[kind, source],
            device_id=(source, d), device_id_type=MESH,
        )

    def begin(k, carry):
        send(1, k).start()

        @pl.when(k != g)
        def _():
            send(0, k).start()

        return carry

    for tiles, pieces in ((range(0, 5), range(0, 4)), (range(5, TILES), range(4, GRP))):
        for j in tiles:
            at = slice(j * LANES, (j + 1) * LANES)
            scaled = jnp.where(live, field[at, :] * scale, 0.0).astype(BF16)
            rows = lax.dot_general(slots, scaled, (((1,), (1,)), ((), ())), preferred_element_type=F32)
            stored[j] = rows.astype(BF16).reshape(MAXORB, 2, LANES)
            parts = [rows[8 * i : 8 * i + 8] for i in range(16)]
            parts = [p * p for p in parts]
            while len(parts) > 1:
                parts = [parts[i] + parts[i + 1] for i in range(0, len(parts), 2)]
            dens = parts[0]
            dens = dens + pltpu.roll(dens, 4, 0)
            dens = dens + pltpu.roll(dens, 2, 0)
            patch[:, at] = dens[0:2] * sign
        for k in pieces:
            piece = patch[:, k * SHARE : (k + 1) * SHARE]
            outgoing[0, k] = piece[0:1]
            outgoing[1, k] = piece[1:2]
        lax.fori_loop(pieces[0], pieces[-1] + 1, begin, 0)

    def land(k, carry):
        arrival(1, k).wait_recv()

        @pl.when(k != g)
        def _():
            arrival(0, k).wait_recv()

        return carry

    lax.fori_loop(0, GRP, land, 0)
    incoming[0, g] = outgoing[0, g]
    density[...] = jnp.sum(incoming[0], axis=0) + jnp.sum(incoming[1], axis=0)

    def leave(k, carry):
        send(1, k).wait_send()

        @pl.when(k != g)
        def _():
            send(0, k).wait_send()

        return carry

    lax.fori_loop(0, GRP, leave, 0)
    block.wait_send()

def deliver(share, stored, density, filtered, sem):
    copies = [
        pltpu.make_async_copy(stored.at[j], filtered.at[:, :, pl.ds(j * LANES, LANES)], sem.at[j])
        for j in range(TILES)
    ]
    copies.append(pltpu.make_async_copy(share, density, sem.at[TILES]))
    for copy in copies:
        copy.start()
    for copy in copies:
        copy.wait()


def on_device(orbitals, potential, counts, parity):
    vmem = pl.BlockSpec(memory_space=pltpu.VMEM)
    hbm = pl.BlockSpec(memory_space=pl.ANY)
    share, stored = pl.pallas_call(
        kernel,
        in_specs=[pl.BlockSpec(memory_space=pltpu.HBM)] * 4,
        out_specs=[vmem, vmem],
        out_shape=[
            pltpu.VMEM((1, SHARE), F32),
            pltpu.VMEM((TILES, MAXORB, 2, LANES), BF16),
        ],
        scratch_shapes=[
            pltpu.VMEM((TILES, MAXORB, 2, LANES), BF16),
            pltpu.VMEM((CELLS, LANES), F32),
            pltpu.VMEM((CELLS, LANES), F32),
            pltpu.VMEM((1, CELLS), BF16),
            pltpu.VMEM((1, CELLS), BF16),
            pltpu.VMEM((2, CELLS), F32),
            pltpu.VMEM((2, GRP, 1, SHARE), F32),
            pltpu.VMEM((2, GRP, 1, SHARE), F32),
            pltpu.SMEM((1, DEV), jnp.int32),
            pltpu.SMEM((1, 1), jnp.int32),
            pltpu.SemaphoreType.DMA((TILES,)),
            pltpu.SemaphoreType.DMA((3,)),
            pltpu.SemaphoreType.DMA((2,)),
            pltpu.SemaphoreType.DMA((2, GRP)),
            pltpu.SemaphoreType.DMA((2, GRP)),
        ],
        compiler_params=pltpu.CompilerParams(collective_id=0, has_side_effects=True),
        name="filter_and_assemble",
    )(counts, parity, potential, orbitals[0, 0])
    density, filtered = pl.pallas_call(
        deliver,
        in_specs=[vmem, vmem],
        out_specs=[hbm, hbm],
        out_shape=[
            jax.ShapeDtypeStruct((1, SHARE), F32),
            jax.ShapeDtypeStruct((MAXORB, 2, CELLS), BF16),
        ],
        scratch_shapes=[pltpu.SemaphoreType.DMA((TILES + 1,))],
        name="deliver",
    )(pltpu.with_memory_space_constraint(share, pltpu.VMEM), pltpu.with_memory_space_constraint(stored, pltpu.VMEM))
    return density[None], filtered[None, None]


def solution(mesh):
    placed = (P("grp", "dev", None, None, None), P("dev", None), P("grp", None), P("grp", "dev"))
    return jax.shard_map(
        on_device,
        mesh=mesh,
        in_specs=placed,
        out_specs=(P("dev", None, "grp"), P("grp", "dev", None, None, None)),
        check_vma=False,
    )
```
